32 devices in a mesh: gr: 4 (over z), gc: 8 (over y, x, core).
Axes of the slice: x: 2, y: 2, z: 4, core: 2. Of those that a mesh axis runs over, the one named last changes fastest.
Arguments:
- student: bfloat16 [4096, 1024], P(('gr', 'gc')), may hold values from -500 to 500
- teacher: bfloat16 [4096, 1024], P(('gr', 'gc')), may hold values from -500 to 500
Outputs:
- student_grad: float32 [4096, 1024], P(('gr', 'gc'))
The draws below stay inside these ranges and needn't reach their ends.
All inputs are finite; a program needn't handle non-finite values.
Results may differ from the reference program's by a relative error of at most 0.0085.
Values may be sent and summed in bfloat16 or wider, within the bound.
No kernel may reach another device: no remote copies, remote signals or barrier semaphores. Data moves between devices by JAX's collectives and lax.ppermute only.
A program may use at most 64 MiB of HBM per device.

```python
import math
import jax
import jax.numpy as jnp
from jax import lax

D = 1024
ROWS = 4096
N_GR = 4


def embed_draw(key, salt):
    key = jax.random.fold_in(key, salt)
    key_base, key_rows, key_cols = jax.random.split(key, 3)
    base = jnp.clip(jax.random.normal(key_base, (ROWS, D), jnp.float32), -4.0, 4.0)
    row_scale = jnp.exp(jax.random.uniform(key_rows, (ROWS, 1), jnp.float32, 0.0, math.log(10.0)))
    col_scale = jnp.exp(jax.random.uniform(key_cols, (1, D), jnp.float32, 0.0, math.log(10.0)))
    return (base * row_scale * col_scale).astype(jnp.bfloat16)


def draw_student(key, part):
    return embed_draw(key, 11)


def draw_teacher(key, part):
    return embed_draw(key, 29)


def setup_inputs(seed: int = 0) -> dict:
    key_of = jax.random.split(jax.random.key(seed), 3)
    return {
        "student": draw_student(jax.random.fold_in(key_of[2], 71), 0),
        "teacher": draw_teacher(jax.random.fold_in(key_of[2], 71), 0),
    }


def unit_rows(embedded):
    values = embedded.astype(jnp.float32)
    inverse_rms = lax.rsqrt(lax.optimization_barrier(jnp.mean(values * values, axis=-1, keepdims=True)) + 1e-06)
    unit = (values * inverse_rms * D ** (-0.5)).astype(jnp.bfloat16)
    return (unit, inverse_rms)

def reference(student, teacher):
    unit_s, inv_s = unit_rows(student)
    unit_t, inv_t = unit_rows(teacher)
    block_s = unit_s.reshape(N_GR, ROWS // N_GR, D)
    block_t = unit_t.reshape(N_GR, ROWS // N_GR, D)
    stretch = 0.5 * D ** 0.5

    def one_block(blocks):
        rows_s, rows_t = blocks
        sim_student = lax.dot_general(rows_s, unit_s, (((1,), (1,)), ((), ())), preferred_element_type=jnp.float32)
        sim_teacher = lax.dot_general(rows_t, unit_t, (((1,), (1,)), ((), ())), preferred_element_type=jnp.float32)
        mismatch = jnp.tanh(stretch * (sim_student - sim_teacher)).astype(jnp.bfloat16)
        return jnp.dot(mismatch, unit_s, preferred_element_type=jnp.float32)
    pull = lax.map(one_block, (block_s, block_t)).reshape(ROWS, D)
    unit_float = unit_s.astype(jnp.float32)
    radial = lax.optimization_barrier(jnp.sum(unit_float * pull, axis=-1, keepdims=True))
    factor = 12.0 * (D / ROWS) ** 0.5
    return factor * inv_s * (pull - radial * unit_float)
```

```python
import functools

import jax
import jax.numpy as jnp
from jax import lax
from jax.experimental import pallas as pl
from jax.experimental.pallas import tpu as pltpu
from jax.sharding import PartitionSpec as P

F32, BF16 = jnp.float32, jnp.bfloat16
VM = pl.BlockSpec(memory_space=pltpu.VMEM)


def inverse_rms(values):
    return lax.rsqrt(jnp.mean(values * values, axis=-1, keepdims=True) + 1e-06)


def unit_of(rows):
    values = rows.astype(F32)
    return (values * inverse_rms(values) * rows.shape[-1] ** (-0.5)).astype(BF16)


def nt(a, b):
    return lax.dot_general(a, b, (((1,), (1,)), ((), ())), preferred_element_type=F32)


def tn(a, b):
    return lax.dot_general(a, b, (((0,), (0,)), ((), ())), preferred_element_type=F32)


def nn(a, b):
    return lax.dot_general(a, b, (((1,), (0,)), ((), ())), preferred_element_type=F32)


def call(kernel, outs, *args, flops=0):
    size = sum(a.size * a.dtype.itemsize for a in args)
    size += sum(o.size * o.dtype.itemsize for o in outs)
    return pl.pallas_call(
        kernel,
        out_shape=outs,
        in_specs=[VM] * len(args),
        out_specs=[VM] * len(outs),
        cost_estimate=pl.CostEstimate(flops=flops, bytes_accessed=size, transcendentals=0),
        compiler_params=pltpu.CompilerParams(vmem_limit_bytes=56 << 20),
    )(*args)


def shape(rows, cols, dtype):
    return jax.ShapeDtypeStruct((rows, cols), dtype)


def block_kernel(n, *refs):
    raw_s, raw_t = refs[:n], refs[n : 2 * n]
    block_s, block_t, pull = refs[2 * n :]
    rows = raw_s[0].shape[0]
    stretch = 0.5 * raw_s[0].shape[1] ** 0.5
    for k in range(n):
        block_s[pl.ds(k * rows, rows), :] = unit_of(raw_s[k][...])
        block_t[pl.ds(k * rows, rows), :] = unit_of(raw_t[k][...])
    own_s, own_t = block_s[pl.ds(0, rows), :], block_t[pl.ds(0, rows), :]
    sim = nt(own_s, block_s[...]) - nt(own_t, block_t[...])
    mismatch = jnp.tanh(stretch * sim).astype(BF16)
    pull[...] = nn(mismatch, block_s[...])


def pair_kernel(n_once, n_both, chunk, *refs):
    block_s, block_t = refs[:2]
    n = n_once + n_both
    raw_s, raw_t = refs[2 : 2 + n], refs[2 + n : 2 + 2 * n]
    outs = refs[2 + 2 * n :]
    back, keep, send = outs[:n_once], outs[n_once], outs[n_once + 1]
    rows, width = raw_s[0].shape
    stretch = 0.5 * width**0.5
    other_s = jnp.concatenate([unit_of(r[...]) for r in raw_s], axis=0)
    other_t = jnp.concatenate([unit_of(r[...]) for r in raw_t], axis=0)
    total = block_s.shape[0]
    half = total // 2
    sums = [None] * n_once
    for start in range(total - chunk, -1, -chunk):
        piece_s = block_s[pl.ds(start, chunk), :]
        piece_t = block_t[pl.ds(start, chunk), :]
        sim = nt(piece_s, other_s) - nt(piece_t, other_t)
        mismatch = jnp.tanh(stretch * sim).astype(BF16)
        part = nn(mismatch, other_s)
        if start >= half:
            send[pl.ds(start - half, chunk), :] = part.astype(BF16)
        else:
            keep[pl.ds(start, chunk), :] = part
        for i in range(n_once):
            term = tn(mismatch[:, i * rows : (i + 1) * rows], piece_s)
            sums[i] = term if sums[i] is None else sums[i] + term
    for i in range(n_once):
        back[i][...] = sums[i].astype(BF16)


def merge_kernel(keep, came, *outs):
    rows = outs[0].shape[0]
    for k, out in enumerate(outs):
        at = pl.ds(k * rows, rows)
        out[...] = (keep[at, :] + came[at, :].astype(F32)).astype(out.dtype)


def end_kernel(factor, student, *refs):
    terms, out = refs[:-1], refs[-1]
    values = student[...].astype(F32)
    inverse = inverse_rms(values)
    unit = (values * inverse * values.shape[-1] ** (-0.5)).astype(BF16).astype(F32)
    pull = terms[0][...]
    for term in terms[1:]:
        pull = pull + term[...].astype(F32)
    radial = jnp.sum(unit * pull, axis=-1, keepdims=True)
    out[...] = factor * inverse * (pull - radial * unit)


def local(n_gr, n_gc, student, teacher):
    rows, width = student.shape
    axes = ("gr", "gc")

    def shift(x, pairs):
        return lax.ppermute(x, axes, pairs)

    def across(x, mask):
        return shift(
            x,
            [(g * n_gc + c, g * n_gc + (c ^ mask)) for g in range(n_gr) for c in range(n_gc)],
        )

    order = []
    for i in range(n_gr):
        order.append(i // 2 if i % 2 == 0 else n_gr - 1 - i // 2)

    def along(x, step):
        pairs = []
        for i in range(n_gr):
            a, b = order[i], order[(i + step) % n_gr]
            pairs += [(a * n_gc + c, b * n_gc + c) for c in range(n_gc)]
        return shift(x, pairs)

    once = list(range(1, (n_gr + 1) // 2))
    both = [n_gr // 2] if n_gr % 2 == 0 else []
    far_s = [along(student, d) for d in once + both]
    far_t = [along(teacher, d) for d in once + both]

    got_s, got_t = {0: student}, {0: teacher}
    for k in range(2, n_gc, 2):
        high = 1 << (k.bit_length() - 1)
        low = k & -k
        got_s[k] = across(got_s[k ^ high], high)
        got_t[k] = across(got_t[k ^ low], low)
    even = list(range(0, n_gc, 2))
    for k in even:
        got_s[k + 1] = across(got_s[k], 1)
        got_t[k + 1] = across(got_t[k], 1)
    slots = even + [k + 1 for k in even]
    total = rows * n_gc
    block_s, block_t, near = call(
        functools.partial(block_kernel, n_gc),
        [shape(total, width, BF16), shape(total, width, BF16), shape(rows, width, F32)],
        *[got_s[k] for k in slots],
        *[got_t[k] for k in slots],
        flops=6 * rows * total * width,
    )
    n = len(once) + len(both)
    half = total // 2
    outs = call(
        functools.partial(pair_kernel, len(once), len(both), min(256, half)),
        [shape(rows, width, BF16)] * len(once)
        + [shape(half, width, F32), shape(half, width, BF16)],
        block_s,
        block_t,
        *far_s,
        *far_t,
        flops=(6 * n + 2 * len(once)) * rows * total * width,
    )
    back, keep, send = outs[: len(once)], outs[-2], outs[-1]
    home = [along(b, n_gr - d) for b, d in zip(back, once)]
    came = across(send, 1)
    merged = call(
        merge_kernel,
        [shape(rows, width, F32)] + [shape(rows, width, BF16)] * (len(even) - 1),
        keep,
        came,
    )
    terms = [across(m, k) for m, k in zip(merged[1:], even[1:])]
    factor = 12.0 * (width / (rows * n_gr * n_gc)) ** 0.5
    return call(
        functools.partial(end_kernel, factor),
        [shape(rows, width, F32)],
        student,
        near,
        merged[0],
        *terms,
        *home,
    )[0]


def solution(mesh):
    n_gr, n_gc = mesh.shape["gr"], mesh.shape["gc"]
    spec = P(("gr", "gc"), None)
    return jax.shard_map(
        functools.partial(local, n_gr, n_gc),
        mesh=mesh,
        in_specs=(spec, spec),
        out_specs=spec,
        check_vma=False,
    )
```

```python
import functools

import jax
import jax.numpy as jnp
from jax import lax
from jax.experimental import pallas as pl
from jax.experimental.pallas import tpu as pltpu
from jax.sharding import PartitionSpec as P


F32, BF16 = jnp.float32, jnp.bfloat16
VM = pl.BlockSpec(memory_space=pltpu.VMEM)


def inverse_rms(values):
    return lax.rsqrt(jnp.mean(values * values, axis=-1, keepdims=True) + 1e-06)


def unit_of(rows):
    values = rows.astype(F32)
    return (values * inverse_rms(values) * rows.shape[-1] ** (-0.5)).astype(BF16)


def nt(a, b):
    return lax.dot_general(a, b, (((1,), (1,)), ((), ())), preferred_element_type=F32)


def tn(a, b):
    return lax.dot_general(a, b, (((0,), (0,)), ((), ())), preferred_element_type=F32)


def nn(a, b):
    return lax.dot_general(a, b, (((1,), (0,)), ((), ())), preferred_element_type=F32)


def call(kernel, outs, *args, flops=0):
    size = sum(a.size * a.dtype.itemsize for a in args)
    size += sum(o.size * o.dtype.itemsize for o in outs)
    return pl.pallas_call(
        kernel,
        out_shape=outs,
        in_specs=[VM] * len(args),
        out_specs=[VM] * len(outs),
        cost_estimate=pl.CostEstimate(flops=flops, bytes_accessed=size, transcendentals=0),
        compiler_params=pltpu.CompilerParams(vmem_limit_bytes=24 << 20),
    )(*args)


def shape(rows, cols, dtype):
    return jax.ShapeDtypeStruct((rows, cols), dtype)


def block_kernel(n, *refs):
    raw_s, raw_t = refs[:n], refs[n : 2 * n]
    block_s, block_t, pull = refs[2 * n :]
    rows = raw_s[0].shape[0]
    stretch = 0.5 * raw_s[0].shape[1] ** 0.5
    for k in range(n):
        block_s[pl.ds(k * rows, rows), :] = unit_of(raw_s[k][...])
        block_t[pl.ds(k * rows, rows), :] = unit_of(raw_t[k][...])
    own_s, own_t = block_s[pl.ds(0, rows), :], block_t[pl.ds(0, rows), :]
    sim = nt(own_s, block_s[...]) - nt(own_t, block_t[...])
    mismatch = jnp.tanh(stretch * sim).astype(BF16)
    pull[...] = nn(mismatch, block_s[...])


def pair_kernel(n_once, n_both, chunk, *refs):
    block_s, block_t = refs[:2]
    n = n_once + n_both
    raw_s, raw_t = refs[2 : 2 + n], refs[2 + n : 2 + 2 * n]
    outs = refs[2 + 2 * n :]
    back, keep, send = outs[:n_once], outs[n_once], outs[n_once + 1]
    rows, width = raw_s[0].shape
    stretch = 0.5 * width**0.5
    other_s = jnp.concatenate([unit_of(r[...]) for r in raw_s], axis=0)
    other_t = jnp.concatenate([unit_of(r[...]) for r in raw_t], axis=0)
    total = block_s.shape[0]
    half = total // 2
    sums = [None] * n_once
    for start in range(total - chunk, -1, -chunk):
        piece_s = block_s[pl.ds(start, chunk), :]
        piece_t = block_t[pl.ds(start, chunk), :]
        sim = nt(piece_s, other_s) - nt(piece_t, other_t)
        mismatch = jnp.tanh(stretch * sim).astype(BF16)
        part = nn(mismatch, other_s)
        if start >= half:
            send[pl.ds(start - half, chunk), :] = part.astype(BF16)
        else:
            keep[pl.ds(start, chunk), :] = part
        for i in range(n_once):
            term = tn(mismatch[:, i * rows : (i + 1) * rows], piece_s)
            sums[i] = term if sums[i] is None else sums[i] + term
    for i in range(n_once):
        back[i][...] = sums[i].astype(BF16)


def merge_kernel(keep, came, *outs):
    rows = outs[0].shape[0]
    for k, out in enumerate(outs):
        at = pl.ds(k * rows, rows)
        out[...] = (keep[at, :] + came[at, :].astype(F32)).astype(out.dtype)


def end_kernel(factor, student, *refs):
    terms, out = refs[:-1], refs[-1]
    values = student[...].astype(F32)
    inverse = inverse_rms(values)
    unit = (values * inverse * values.shape[-1] ** (-0.5)).astype(BF16).astype(F32)
    pull = terms[0][...]
    for term in terms[1:]:
        pull = pull + term[...].astype(F32)
    radial = jnp.sum(unit * pull, axis=-1, keepdims=True)
    out[...] = factor * inverse * (pull - radial * unit)


def local(n_gr, n_gc, student, teacher):
    rows, width = student.shape
    axes = ("gr", "gc")

    def shift(x, pairs):
        return lax.ppermute(x, axes, pairs)

    def across(x, mask):
        pairs = [(g * n_gc + c, g * n_gc + (c ^ mask)) for g in range(n_gr) for c in range(n_gc)]
        return shift(x, pairs)

    order = []
    for i in range(n_gr):
        order.append(i // 2 if i % 2 == 0 else n_gr - 1 - i // 2)

    def along(x, step):
        pairs = []
        for i in range(n_gr):
            a, b = order[i], order[(i + step) % n_gr]
            pairs += [(a * n_gc + c, b * n_gc + c) for c in range(n_gc)]
        return shift(x, pairs)

    once = list(range(1, (n_gr + 1) // 2))
    both = [n_gr // 2] if n_gr % 2 == 0 else []
    far_s = [along(student, d) for d in once + both]
    far_t = [along(teacher, d) for d in once + both]

    got_s, got_t = {0: student}, {0: teacher}
    for k in range(2, n_gc, 2):
        high = 1 << (k.bit_length() - 1)
        low = k & -k
        got_s[k] = across(got_s[k ^ high], high)
        got_t[k] = across(got_t[k ^ low], low)
    even = list(range(0, n_gc, 2))
    for k in even:
        got_s[k + 1] = across(got_s[k], 1)
        got_t[k + 1] = across(got_t[k], 1)
    slots = even + [k + 1 for k in even]
    total = rows * n_gc
    block_s, block_t, near = call(
        functools.partial(block_kernel, n_gc),
        [shape(total, width, BF16), shape(total, width, BF16), shape(rows, width, F32)],
        *[got_s[k] for k in slots],
        *[got_t[k] for k in slots],
        flops=6 * rows * total * width,
    )
    n = len(once) + len(both)
    half = total // 2
    outs = call(
        functools.partial(pair_kernel, len(once), len(both), min(256, half)),
        [shape(rows, width, BF16)] * len(once)
        + [shape(half, width, F32), shape(half, width, BF16)],
        block_s,
        block_t,
        *far_s,
        *far_t,
        flops=(6 * n + 2 * len(once)) * rows * total * width,
    )
    back, keep, send = outs[: len(once)], outs[-2], outs[-1]
    home = [along(b, n_gr - d) for b, d in zip(back, once)]
    came = across(send, 1)
    merged = call(
        merge_kernel,
        [shape(rows, width, F32)] + [shape(rows, width, BF16)] * (len(even) - 1),
        keep,
        came,
    )
    terms = [across(m, k) for m, k in zip(merged[1:], even[1:])]
    factor = 12.0 * (width / (rows * n_gr * n_gc)) ** 0.5
    return call(
        functools.partial(end_kernel, factor),
        [shape(rows, width, F32)],
        student,
        near,
        merged[0],
        *terms,
        *home,
    )[0]


def solution(mesh):
    n_gr, n_gc = mesh.shape["gr"], mesh.shape["gc"]
    spec = P(("gr", "gc"), None)

    def body(student, teacher):
        return local(n_gr, n_gc, student, teacher)

    return jax.shard_map(
        body, mesh=mesh, in_specs=(spec, spec), out_specs=spec, check_vma=False
    )
```

```python
import functools

import jax
import jax.numpy as jnp
from jax import lax
from jax.experimental import pallas as pl
from jax.experimental.pallas import tpu as pltpu
from jax.sharding import PartitionSpec as P


F32, BF16 = jnp.float32, jnp.bfloat16
VM = pl.BlockSpec(memory_space=pltpu.VMEM)


def inverse_rms(values):
    return lax.rsqrt(jnp.mean(values * values, axis=-1, keepdims=True) + 1e-06)


def unit_of(rows):
    values = rows.astype(F32)
    return (values * inverse_rms(values) * rows.shape[-1] ** (-0.5)).astype(BF16)


def nt(a, b):
    return lax.dot_general(a, b, (((1,), (1,)), ((), ())), preferred_element_type=F32)


def tn(a, b):
    return lax.dot_general(a, b, (((0,), (0,)), ((), ())), preferred_element_type=F32)


def nn(a, b):
    return lax.dot_general(a, b, (((1,), (0,)), ((), ())), preferred_element_type=F32)


def call(kernel, outs, *args, flops=0):
    size = sum(a.size * a.dtype.itemsize for a in args)
    size += sum(o.size * o.dtype.itemsize for o in outs)
    return pl.pallas_call(
        kernel,
        out_shape=outs,
        in_specs=[VM] * len(args),
        out_specs=[VM] * len(outs),
        cost_estimate=pl.CostEstimate(flops=flops, bytes_accessed=size, transcendentals=0),
        compiler_params=pltpu.CompilerParams(vmem_limit_bytes=24 << 20),
    )(*args)


def shape(rows, cols, dtype):
    return jax.ShapeDtypeStruct((rows, cols), dtype)


def store_units(outs, raws):
    n = len(raws) // len(outs)
    for i, raw in enumerate(raws):
        rows = raw.shape[0]
        outs[i // n][pl.ds(i % n * rows, rows), :] = unit_of(raw[...])


def pull_of(rows_s, rows_t, *block):
    stretch = 0.5 * rows_s.shape[1] ** 0.5
    total = None
    for piece_s, piece_t in zip(block[::2], block[1::2]):
        sim = nt(rows_s, piece_s[...]) - nt(rows_t, piece_t[...])
        term = nn(jnp.tanh(stretch * sim).astype(BF16), piece_s[...])
        total = term if total is None else total + term
    return total


def own_kernel(student, teacher, unit_s, unit_t, scale):
    values = student[...].astype(F32)
    inverse = inverse_rms(values)
    unit_s[...] = (values * inverse * values.shape[-1] ** (-0.5)).astype(BF16)
    unit_t[...] = unit_of(teacher[...])
    scale[...] = jnp.broadcast_to(inverse, scale.shape)


def early_kernel(own_s, own_t, *refs):
    *raws, early_s, early_t, pull = refs
    rows = own_s.shape[0]
    more = early_s.shape[0] - rows
    early_s[pl.ds(0, rows), :] = own_s[...]
    early_t[pl.ds(0, rows), :] = own_t[...]
    at = pl.ds(rows, more)
    store_units((early_s.at[at, :], early_t.at[at, :]), raws)
    pull[...] = pull_of(own_s[...], own_t[...], early_s, early_t)


def mid_kernel(own_s, own_t, before, *refs):
    *raws, mid_s, mid_t, pull = refs
    store_units((mid_s, mid_t), raws)
    pull[...] = before[...] + pull_of(own_s[...], own_t[...], mid_s, mid_t)


def lift_kernel(early_s, mid_s, *refs):
    *raws, once_s, early_p, mid_p = refs
    store_units((once_s,), raws)
    early_p[...] = nt(early_s[...], once_s[...])
    mid_p[...] = nt(mid_s[...], once_s[...])


def late_kernel(once_s, *refs):
    *raws, late_s, late_t, late_p = refs
    store_units((late_s, late_t), raws)
    late_p[...] = nt(late_s[...], once_s[...])


def once_kernel(early_t, mid_t, late_t, early_p, mid_p, late_p, *refs):
    *raws, kept, sent = refs
    stretch = 0.5 * early_t.shape[1] ** 0.5
    once_t = jnp.concatenate([unit_of(r[...]) for r in raws], axis=0)
    first = early_t.shape[0]
    skip = kept.shape[0] - first
    for piece, product, out in (
        (mid_t[...], mid_p[...], sent.at[pl.ds(0, first), :]),
        (early_t[...], early_p[...], kept.at[pl.ds(0, first), :]),
    ):
        out[...] = jnp.tanh(stretch * (product - nt(piece, once_t))).astype(BF16)
    part = jnp.tanh(stretch * (late_p[...] - nt(late_t[...], once_t))).astype(BF16)
    kept[pl.ds(first, skip), :] = part[:skip]
    sent[pl.ds(first, skip), :] = part[skip:]


def back_kernel(early_s, mid_s, late_s, kept, sent, *back):
    first = early_s.shape[0]
    skip = kept.shape[0] - first
    sums = tn(kept[pl.ds(0, first), :], early_s[...]) + tn(sent[pl.ds(0, first), :], mid_s[...])
    last = jnp.concatenate([kept[pl.ds(first, skip), :], sent[pl.ds(first, skip), :]], axis=0)
    sums += tn(last, late_s[...])
    rows = back[0].shape[0]
    for i, out in enumerate(back):
        out[...] = sums[i * rows : (i + 1) * rows].astype(BF16)


def both_kernel(n_both, *refs):
    block, raw_s, raw_t, back = refs[:6], refs[6 : 6 + n_both], refs[6 + n_both : -n_both], refs[-n_both:]
    for i in range(n_both):
        back[i][...] = pull_of(unit_of(raw_s[i][...]), unit_of(raw_t[i][...]), *block).astype(BF16)


def near_kernel(own_s, own_t, late_s, late_t, before, pull):
    pull[...] = before[...] + pull_of(own_s[...], own_t[...], late_s, late_t)


def pack_kernel(kept, came, *outs):
    rows, cols = outs[0].shape
    for k, out in enumerate(outs):
        at = pl.ds(k * rows, rows)
        out[:, pl.ds(0, cols // 2)] = kept[at, :]
        out[:, pl.ds(cols // 2, cols // 2)] = came[at, :]


def met_kernel(n, before, *refs):
    weights, units, pull = refs[:n], refs[n:-1], refs[-1]
    total = before[...]
    for k, weight in enumerate(weights):
        block = jnp.concatenate([units[2 * k][...], units[2 * k + 1][...]], axis=0)
        total += nn(weight[...], block)
    pull[...] = total


def end_kernel(factor, own_s, scale, *refs):
    *terms, out = refs
    unit = own_s[...].astype(F32)
    pull = terms[0][...]
    for term in terms[1:]:
        pull = pull + term[...].astype(F32)
    radial = jnp.sum(unit * pull, axis=-1, keepdims=True)
    out[...] = factor * scale[:, :1] * (pull - radial * unit)


def local(n_gr, n_gc, student, teacher):
    rows, width = student.shape
    axes = ("gr", "gc")

    def shift(x, pairs):
        return lax.ppermute(x, axes, pairs)

    def across(x, mask):
        pairs = [(g * n_gc + c, g * n_gc + (c ^ mask)) for g in range(n_gr) for c in range(n_gc)]
        return shift(x, pairs)

    order = []
    for i in range(n_gr):
        order.append(i // 2 if i % 2 == 0 else n_gr - 1 - i // 2)

    def along(x, step):
        pairs = []
        for i in range(n_gr):
            a, b = order[i], order[(i + step) % n_gr]
            pairs += [(a * n_gc + c, b * n_gc + c) for c in range(n_gc)]
        return shift(x, pairs)

    def run(kernel, outs, *args, flops=0):
        return call(kernel, outs, *args, flops=flops)

    once = list(range(1, (n_gr + 1) // 2))
    both = [n_gr // 2] if n_gr % 2 == 0 else []
    n_once, n_both = len(once), len(both)
    once_rows = n_once * rows
    far_s = [along(student, d) for d in once + both]
    far_t = [along(teacher, d) for d in once + both]

    even = list(range(0, n_gc, 2))
    early = [k for k in even if k & (k - 1) == 0]
    late = [k for k in even if k not in early]
    mid = [k + 1 for k in early]
    last = late + [k + 1 for k in late]
    half = rows * len(even)
    work = 2 * rows * width

    got_s, got_t = {0: student}, {0: teacher}
    for k in even[1:]:
        high = 1 << (k.bit_length() - 1)
        low = k & -k
        got_s[k] = across(got_s[k ^ high], high)
        got_t[k] = across(got_t[k ^ low], low)
    for k in even:
        got_s[k + 1] = across(got_s[k], 1)
        got_t[k + 1] = across(got_t[k], 1)

    def raws(slots):
        return [got_s[k] for k in slots] + [got_t[k] for k in slots]

    pull_shape = shape(rows, width, F32)
    own_s, own_t, scale = run(
        own_kernel, [shape(rows, width, BF16)] * 2 + [shape(rows, 128, F32)], student, teacher
    )
    early_s, early_t, pull = run(
        early_kernel,
        [shape(len(early) * rows, width, BF16)] * 2 + [pull_shape],
        own_s,
        own_t,
        *raws(early[1:]),
        flops=3 * len(early) * rows * work,
    )
    mid_s, mid_t, pull = run(
        mid_kernel,
        [shape(len(mid) * rows, width, BF16)] * 2 + [pull_shape],
        own_s,
        own_t,
        pull,
        *raws(mid),
        flops=3 * len(mid) * rows * work,
    )

    once_s, early_p, mid_p = run(
        lift_kernel,
        [shape(once_rows, width, BF16)] + [shape(len(early) * rows, once_rows, F32)] * 2,
        early_s,
        mid_s,
        *far_s[:n_once],
        flops=2 * len(early) * once_rows * work,
    )
    mates = {0: once_s}
    for k in even[1:]:
        mates[k] = across(once_s, k)
    for k in even:
        mates[k + 1] = across(mates[k], 1)

    late_s, late_t, late_p = run(
        late_kernel,
        [shape(len(last) * rows, width, BF16)] * 2 + [shape(len(last) * rows, once_rows, F32)],
        once_s,
        *raws(last),
        flops=len(last) * once_rows * work,
    )
    kept, sent = run(
        once_kernel,
        [shape(half, once_rows, BF16)] * 2,
        early_t,
        mid_t,
        late_t,
        early_p,
        mid_p,
        late_p,
        *far_t[:n_once],
        flops=n_gc * once_rows * work,
    )
    came = across(sent, 1)
    back = run(
        back_kernel,
        [shape(rows, width, BF16)] * n_once,
        early_s,
        mid_s,
        late_s,
        kept,
        sent,
        flops=n_gc * once_rows * work,
    )
    home = [along(b, n_gr - d) for b, d in zip(back, once)]
    packed = run(pack_kernel, [shape(rows, 2 * once_rows, BF16)] * len(even), kept, came)
    order_of = early + late
    weights = [packed[0]] + [across(p, k) for p, k in zip(packed[1:], order_of[1:])]
    back = run(
        functools.partial(both_kernel, n_both),
        [shape(rows, width, BF16)] * n_both,
        early_s,
        early_t,
        mid_s,
        mid_t,
        late_s,
        late_t,
        *far_s[n_once:],
        *far_t[n_once:],
        flops=3 * n_both * n_gc * rows * work,
    )
    home += [along(b, n_gr - d) for b, d in zip(back, both)]
    (pull,) = run(
        near_kernel,
        [pull_shape],
        own_s,
        own_t,
        late_s,
        late_t,
        pull,
        flops=3 * len(last) * rows * work,
    )
    (pull,) = run(
        functools.partial(met_kernel, len(even)),
        [pull_shape],
        pull,
        *weights,
        *[mates[k + c] for k in order_of for c in (0, 1)],
        flops=n_gc * once_rows * work,
    )
    factor = 12.0 * (width / (rows * n_gr * n_gc)) ** 0.5
    return run(functools.partial(end_kernel, factor), [pull_shape], own_s, scale, pull, *home)[0]


def solution(mesh):
    n_gr, n_gc = mesh.shape["gr"], mesh.shape["gc"]
    spec = P(("gr", "gc"), None)

    def body(student, teacher):
        return local(n_gr, n_gc, student, teacher)

    return jax.shard_map(
        body, mesh=mesh, in_specs=(spec, spec), out_specs=spec, check_vma=False
    )
```

```python
import functools

import jax
import jax.numpy as jnp
from jax import lax
from jax.experimental import pallas as pl
from jax.experimental.pallas import tpu as pltpu
from jax.sharding import PartitionSpec as P


F32, BF16 = jnp.float32, jnp.bfloat16
VM = pl.BlockSpec(memory_space=pltpu.VMEM)


def inverse_rms(values):
    return lax.rsqrt(jnp.mean(values * values, axis=-1, keepdims=True) + 1e-06)


def unit_of(rows):
    values = rows.astype(F32)
    return (values * inverse_rms(values) * rows.shape[-1] ** (-0.5)).astype(BF16)


def nt(a, b):
    return lax.dot_general(a, b, (((1,), (1,)), ((), ())), preferred_element_type=F32)


def tn(a, b):
    return lax.dot_general(a, b, (((0,), (0,)), ((), ())), preferred_element_type=F32)


def nn(a, b):
    return lax.dot_general(a, b, (((1,), (0,)), ((), ())), preferred_element_type=F32)


def call(kernel, outs, *args, flops=0, into=()):
    size = sum(a.size * a.dtype.itemsize for a in args)
    size += sum(o.size * o.dtype.itemsize for o in outs)
    return pl.pallas_call(
        kernel,
        out_shape=outs,
        in_specs=[VM] * len(args),
        out_specs=[VM] * len(outs),
        input_output_aliases={i: i for i in into},
        cost_estimate=pl.CostEstimate(flops=flops, bytes_accessed=size, transcendentals=0),
        compiler_params=pltpu.CompilerParams(vmem_limit_bytes=24 << 20),
    )(*args)


def shape(rows, cols, dtype):
    return jax.ShapeDtypeStruct((rows, cols), dtype)


def store_units(out, starts, raws):
    for at, raw in zip(starts, raws):
        out[pl.ds(at, raw.shape[0]), :] = unit_of(raw[...])


def pull_of(rows_s, rows_t, block_s, block_t):
    stretch = 0.5 * rows_s.shape[1] ** 0.5
    total = None
    half = block_s.shape[0] // 2
    for i in range(2):
        at = pl.ds(i * half, half)
        sim = nt(block_s[at, :], rows_s) - nt(block_t[at, :], rows_t)
        term = tn(jnp.tanh(stretch * sim).astype(BF16), block_s[at, :])
        total = term if total is None else total + term
    return total


def own_kernel(student, teacher, unit_s, unit_t, scale):
    values = student[...].astype(F32)
    inverse = inverse_rms(values)
    unit_s[...] = (values * inverse * values.shape[-1] ** (-0.5)).astype(BF16)
    unit_t[...] = unit_of(teacher[...])
    scale[...] = jnp.broadcast_to(inverse, scale.shape)


def early_kernel(starts, own_s, own_t, *refs):
    *raws, block_s, block_t = refs
    n = len(starts)
    block_s[pl.ds(0, own_s.shape[0]), :] = own_s[...]
    block_t[pl.ds(0, own_s.shape[0]), :] = own_t[...]
    store_units(block_s, starts, raws[:n])
    store_units(block_t, starts, raws[n:])


def lift_kernel(size, block_s, *refs):
    *raws, once_s, product = refs
    rows = raws[0].shape[0]
    store_units(once_s, range(0, len(raws) * rows, rows), raws)
    at = pl.ds(0, size)
    product[at, :] = nt(block_s[at, :], once_s[...])


def more_kernel(starts, block_s, block_t, product, once_s, *refs):
    *raws, out_s, out_t, out = refs
    n = len(starts)
    rows = raws[0].shape[0]
    units = jnp.concatenate([unit_of(r[...]) for r in raws[:n]], axis=0)
    part = nt(units, once_s[...])
    for i, start in enumerate(starts):
        out_s[pl.ds(start, rows), :] = units[i * rows : (i + 1) * rows]
        out[pl.ds(start, rows), :] = part[i * rows : (i + 1) * rows]
    store_units(out_t, starts, raws[n:])


def once_kernel(block_t, product, *refs):
    *raws, kept, sent = refs
    stretch = 0.5 * block_t.shape[1] ** 0.5
    once_t = jnp.concatenate([unit_of(r[...]) for r in raws], axis=0)
    half = kept.shape[0]
    for start, out in ((half, sent), (0, kept)):
        at = pl.ds(start, half)
        sim = product[at, :] - nt(block_t[at, :], once_t)
        out[...] = jnp.tanh(stretch * sim).astype(BF16)


def back_kernel(block_s, kept, sent, *back):
    half = kept.shape[0]
    sums = tn(kept[...], block_s[pl.ds(0, half), :]) + tn(sent[...], block_s[pl.ds(half, half), :])
    rows = back[0].shape[0]
    for i, out in enumerate(back):
        out[...] = sums[i * rows : (i + 1) * rows].astype(BF16)


def both_kernel(n_both, block_s, block_t, *refs):
    raw_s, raw_t, back = refs[:n_both], refs[n_both : 2 * n_both], refs[2 * n_both :]
    for i in range(n_both):
        rows_s, rows_t = unit_of(raw_s[i][...]), unit_of(raw_t[i][...])
        back[i][...] = pull_of(rows_s, rows_t, block_s, block_t).astype(BF16)


def near_kernel(own_s, own_t, block_s, block_t, pull):
    pull[...] = pull_of(own_s[...], own_t[...], block_s, block_t)


def pack_kernel(n_pack, kept, came, once_s, mate_s, *outs):
    rows, half = outs[-1].shape[0], kept.shape[1]
    for k, out in enumerate(outs):
        at = pl.ds(k * rows, rows)
        if k < n_pack:
            out[:, pl.ds(0, half)] = kept[at, :]
            out[:, pl.ds(half, half)] = came[at, :]
        else:
            out[...] = (nn(kept[at, :], once_s[...]) + nn(came[at, :], mate_s[...])).astype(BF16)


def met_kernel(n, before, *refs):
    weights, units, pull = refs[:n], refs[n:-1], refs[-1]
    total = before[...]
    for k, weight in enumerate(weights):
        block = jnp.concatenate([units[2 * k][...], units[2 * k + 1][...]], axis=0)
        total += nn(weight[...], block)
    pull[...] = total


def end_kernel(factor, own_s, scale, *refs):
    *terms, out = refs
    unit = own_s[...].astype(F32)
    pull = terms[0][...]
    for term in terms[1:]:
        pull = pull + term[...].astype(F32)
    radial = jnp.sum(unit * pull, axis=-1, keepdims=True)
    out[...] = factor * scale[:, :1] * (pull - radial * unit)


def local(n_gr, n_gc, student, teacher):
    rows, width = student.shape
    axes = ("gr", "gc")

    def shift(x, pairs):
        return lax.ppermute(x, axes, pairs)

    def across(x, mask):
        pairs = [(g * n_gc + c, g * n_gc + (c ^ mask)) for g in range(n_gr) for c in range(n_gc)]
        return shift(x, pairs)

    order = []
    for i in range(n_gr):
        order.append(i // 2 if i % 2 == 0 else n_gr - 1 - i // 2)

    def along(x, step):
        pairs = []
        for i in range(n_gr):
            a, b = order[i], order[(i + step) % n_gr]
            pairs += [(a * n_gc + c, b * n_gc + c) for c in range(n_gc)]
        return shift(x, pairs)

    def run(kernel, outs, *args, flops=0, into=()):
        return call(kernel, outs, *args, flops=flops, into=into)

    once = list(range(1, (n_gr + 1) // 2))
    both = [n_gr // 2] if n_gr % 2 == 0 else []
    n_once, n_both = len(once), len(both)
    once_rows = n_once * rows
    far_s = [along(student, d) for d in once + both]
    far_t = [along(teacher, d) for d in once + both]

    even = list(range(0, n_gc, 2))
    early = [k for k in even if k & (k - 1) == 0]
    late = [k for k in even if k not in early]
    mid = [k + 1 for k in early]
    last = late + [k + 1 for k in late]
    half = rows * len(even)
    work = 2 * rows * width

    got_s, got_t = {0: student}, {0: teacher}
    for k in even[1:]:
        high = 1 << (k.bit_length() - 1)
        low = k & -k
        got_s[k] = across(got_s[k ^ high], high)
        got_t[k] = across(got_t[k ^ low], low)
    for k in even:
        got_s[k + 1] = across(got_s[k], 1)
        got_t[k + 1] = across(got_t[k], 1)

    def raws(slots):
        return [got_s[k] for k in slots] + [got_t[k] for k in slots]

    order_of = early + late
    place = {k: i * rows for i, k in enumerate(order_of + [k + 1 for k in order_of])}

    def starts(slots):
        return [place[k] for k in slots]

    total = n_gc * rows
    pull_shape = shape(rows, width, F32)
    block_shape = shape(total, width, BF16)
    own_s, own_t, scale = run(
        own_kernel, [shape(rows, width, BF16)] * 2 + [shape(rows, 128, F32)], student, teacher
    )
    block_s, block_t = run(
        functools.partial(early_kernel, starts(early[1:])),
        [block_shape] * 2,
        own_s,
        own_t,
        *raws(early[1:]),
    )
    once_s, product = run(
        functools.partial(lift_kernel, len(early) * rows),
        [shape(once_rows, width, BF16), shape(total, once_rows, F32)],
        block_s,
        *far_s[:n_once],
        flops=len(early) * once_rows * work,
    )
    mates = {k: across(once_s, k) for k in early[1:]}
    mates[0] = once_s
    for k in early:
        mates[k + 1] = across(mates[k], 1)

    for slots in (mid, last):
        block_s, block_t, product = run(
            functools.partial(more_kernel, starts(slots)),
            [block_shape, block_shape, shape(total, once_rows, F32)],
            block_s,
            block_t,
            product,
            once_s,
            *raws(slots),
            flops=len(slots) * once_rows * work,
            into=(0, 1, 2),
        )
    kept, sent = run(
        once_kernel,
        [shape(half, once_rows, BF16)] * 2,
        block_t,
        product,
        *far_t[:n_once],
        flops=n_gc * once_rows * work,
    )
    came = across(sent, 1)
    back = run(
        back_kernel,
        [shape(rows, width, BF16)] * n_once,
        block_s,
        kept,
        sent,
        flops=n_gc * once_rows * work,
    )
    home = [along(b, n_gr - d) for b, d in zip(back, once)]
    n_pack = len(early)
    packed = run(
        functools.partial(pack_kernel, n_pack),
        [shape(rows, 2 * once_rows, BF16)] * n_pack + [shape(rows, width, BF16)] * len(late),
        kept,
        came,
        once_s,
        mates[1],
        flops=len(late) * 2 * once_rows * work,
    )
    weights = [packed[0]] + [across(p, k) for p, k in zip(packed[1:], early[1:])]
    home += [across(p, k) for p, k in zip(packed[n_pack:], late)]
    back = run(
        functools.partial(both_kernel, n_both),
        [shape(rows, width, BF16)] * n_both,
        block_s,
        block_t,
        *far_s[n_once:],
        *far_t[n_once:],
        flops=3 * n_both * n_gc * rows * work,
    )
    home += [along(b, n_gr - d) for b, d in zip(back, both)]
    (pull,) = run(
        near_kernel, [pull_shape], own_s, own_t, block_s, block_t, flops=3 * n_gc * rows * work
    )
    (pull,) = run(
        functools.partial(met_kernel, n_pack),
        [pull_shape],
        pull,
        *weights,
        *[mates[k + c] for k in early for c in (0, 1)],
        flops=n_gc * once_rows * work,
    )
    factor = 12.0 * (width / (rows * n_gr * n_gc)) ** 0.5
    return run(functools.partial(end_kernel, factor), [pull_shape], own_s, scale, pull, *home)[0]


def solution(mesh):
    n_gr, n_gc = mesh.shape["gr"], mesh.shape["gc"]
    spec = P(("gr", "gc"), None)

    def body(student, teacher):
        return local(n_gr, n_gc, student, teacher)

    return jax.shard_map(
        body, mesh=mesh, in_specs=(spec, spec), out_specs=spec, check_vma=False
    )
```

```python
import functools

import jax
import jax.numpy as jnp
from jax import lax
from jax.experimental import pallas as pl
from jax.experimental.pallas import tpu as pltpu
from jax.sharding import PartitionSpec as P


F32, BF16 = jnp.float32, jnp.bfloat16
VM = pl.BlockSpec(memory_space=pltpu.VMEM)


def inverse_rms(values):
    return lax.rsqrt(jnp.mean(values * values, axis=-1, keepdims=True) + 1e-06)


def unit_of(rows):
    values = rows.astype(F32)
    return (values * inverse_rms(values) * rows.shape[-1] ** (-0.5)).astype(BF16)


def nt(a, b):
    return lax.dot_general(a, b, (((1,), (1,)), ((), ())), preferred_element_type=F32)


def tn(a, b):
    return lax.dot_general(a, b, (((0,), (0,)), ((), ())), preferred_element_type=F32)


def nn(a, b):
    return lax.dot_general(a, b, (((1,), (0,)), ((), ())), preferred_element_type=F32)


def call(kernel, outs, *args, flops=0, into=()):
    size = sum(a.size * a.dtype.itemsize for a in args)
    size += sum(o.size * o.dtype.itemsize for o in outs)
    return pl.pallas_call(
        kernel,
        out_shape=outs,
        in_specs=[VM] * len(args),
        out_specs=[VM] * len(outs),
        input_output_aliases={i: i for i in into},
        cost_estimate=pl.CostEstimate(flops=flops, bytes_accessed=size, transcendentals=0),
        compiler_params=pltpu.CompilerParams(vmem_limit_bytes=24 << 20),
    )(*args)


def shape(rows, cols, dtype):
    return jax.ShapeDtypeStruct((rows, cols), dtype)


def store_units(out, starts, raws):
    for at, raw in zip(starts, raws):
        out[pl.ds(at, raw.shape[0]), :] = unit_of(raw[...])


def pull_of(rows_s, rows_t, block_s, block_t):
    stretch = 0.5 * rows_s.shape[1] ** 0.5
    total = None
    half = block_s.shape[0] // 2
    for i in range(2):
        at = pl.ds(i * half, half)
        sim = nt(block_s[at, :], rows_s) - nt(block_t[at, :], rows_t)
        term = tn(jnp.tanh(stretch * sim).astype(BF16), block_s[at, :])
        total = term if total is None else total + term
    return total


def own_kernel(student, teacher, unit_s, unit_t, scale):
    values = student[...].astype(F32)
    inverse = inverse_rms(values)
    unit_s[...] = (values * inverse * values.shape[-1] ** (-0.5)).astype(BF16)
    unit_t[...] = unit_of(teacher[...])
    scale[...] = jnp.broadcast_to(inverse, scale.shape)


def early_kernel(starts, own_s, own_t, *refs):
    *raws, block_s, block_t = refs
    n = len(starts)
    block_s[pl.ds(0, own_s.shape[0]), :] = own_s[...]
    block_t[pl.ds(0, own_s.shape[0]), :] = own_t[...]
    store_units(block_s, starts, raws[:n])
    store_units(block_t, starts, raws[n:])


def lift_kernel(size, block_s, *refs):
    *raws, once_s, product = refs
    rows = raws[0].shape[0]
    store_units(once_s, range(0, len(raws) * rows, rows), raws)
    at = pl.ds(0, size)
    product[at, :] = nt(block_s[at, :], once_s[...])


def more_kernel(starts, block_s, block_t, product, once_s, *refs):
    *raws, out_s, out_t, out = refs
    n = len(starts)
    rows = raws[0].shape[0]
    units = jnp.concatenate([unit_of(r[...]) for r in raws[:n]], axis=0)
    part = nt(units, once_s[...])
    for i, start in enumerate(starts):
        out_s[pl.ds(start, rows), :] = units[i * rows : (i + 1) * rows]
        out[pl.ds(start, rows), :] = part[i * rows : (i + 1) * rows]
    store_units(out_t, starts, raws[n:])


def once_kernel(n_once, block_s, block_t, product, *refs):
    raws, (kept, sent, *back) = refs[:n_once], refs[n_once:]
    stretch = 0.5 * block_t.shape[1] ** 0.5
    once_t = jnp.concatenate([unit_of(r[...]) for r in raws], axis=0)
    half = kept.shape[0]
    sums = None
    for start, out in ((half, sent), (0, kept)):
        at = pl.ds(start, half)
        sim = product[at, :] - nt(block_t[at, :], once_t)
        part = jnp.tanh(stretch * sim).astype(BF16)
        out[...] = part
        term = tn(part, block_s[at, :])
        sums = term if sums is None else sums + term
    rows = back[0].shape[0]
    for i, out in enumerate(back):
        out[...] = sums[i * rows : (i + 1) * rows].astype(BF16)


def both_kernel(n_both, block_s, block_t, *refs):
    raw_s, raw_t, back = refs[:n_both], refs[n_both : 2 * n_both], refs[2 * n_both :]
    for i in range(n_both):
        rows_s, rows_t = unit_of(raw_s[i][...]), unit_of(raw_t[i][...])
        back[i][...] = pull_of(rows_s, rows_t, block_s, block_t).astype(BF16)


def near_kernel(own_s, own_t, block_s, block_t, pull):
    pull[...] = pull_of(own_s[...], own_t[...], block_s, block_t)


def pack_kernel(n_pack, kept, came, once_s, mate_s, *outs):
    rows, half = outs[-1].shape[0], kept.shape[1]
    for k, out in enumerate(outs):
        at = pl.ds(k * rows, rows)
        if k < n_pack:
            out[:, pl.ds(0, half)] = kept[at, :]
            out[:, pl.ds(half, half)] = came[at, :]
        else:
            out[...] = (nn(kept[at, :], once_s[...]) + nn(came[at, :], mate_s[...])).astype(BF16)


def met_kernel(n, before, *refs):
    weights, units, pull = refs[:n], refs[n:-1], refs[-1]
    total = before[...]
    for k, weight in enumerate(weights):
        block = jnp.concatenate([units[2 * k][...], units[2 * k + 1][...]], axis=0)
        total += nn(weight[...], block)
    pull[...] = total


def end_kernel(factor, own_s, scale, *refs):
    *terms, out = refs
    unit = own_s[...].astype(F32)
    pull = terms[0][...]
    for term in terms[1:]:
        pull = pull + term[...].astype(F32)
    radial = jnp.sum(unit * pull, axis=-1, keepdims=True)
    out[...] = factor * scale[:, :1] * (pull - radial * unit)


def local(n_gr, n_gc, student, teacher):
    rows, width = student.shape
    axes = ("gr", "gc")

    def shift(x, pairs):
        return lax.ppermute(x, axes, pairs)

    def across(x, mask):
        pairs = [(g * n_gc + c, g * n_gc + (c ^ mask)) for g in range(n_gr) for c in range(n_gc)]
        return shift(x, pairs)

    order = []
    for i in range(n_gr):
        order.append(i // 2 if i % 2 == 0 else n_gr - 1 - i // 2)

    def along(x, step):
        pairs = []
        for i in range(n_gr):
            a, b = order[i], order[(i + step) % n_gr]
            pairs += [(a * n_gc + c, b * n_gc + c) for c in range(n_gc)]
        return shift(x, pairs)

    def run(kernel, outs, *args, flops=0, into=()):
        return call(kernel, outs, *args, flops=flops, into=into)

    once = list(range(1, (n_gr + 1) // 2))
    both = [n_gr // 2] if n_gr % 2 == 0 else []
    n_once, n_both = len(once), len(both)
    once_rows = n_once * rows
    far_s = [along(student, d) for d in once + both]
    far_t = [along(teacher, d) for d in once + both]

    even = list(range(0, n_gc, 2))
    early = [k for k in even if k & (k - 1) == 0]
    late = [k for k in even if k not in early]
    mid = [k + 1 for k in early]
    last = late + [k + 1 for k in late]
    half = rows * len(even)
    work = 2 * rows * width

    got_s, got_t = {0: student}, {0: teacher}
    for k in even[1:]:
        high = 1 << (k.bit_length() - 1)
        low = k & -k
        got_s[k] = across(got_s[k ^ high], high)
        got_t[k] = across(got_t[k ^ low], low)
    for k in even:
        got_s[k + 1] = across(got_s[k], 1)
        got_t[k + 1] = across(got_t[k], 1)

    def raws(slots):
        return [got_s[k] for k in slots] + [got_t[k] for k in slots]

    order_of = early + late
    place = {k: i * rows for i, k in enumerate(order_of + [k + 1 for k in order_of])}

    def starts(slots):
        return [place[k] for k in slots]

    total = n_gc * rows
    pull_shape = shape(rows, width, F32)
    block_shape = shape(total, width, BF16)
    own_s, own_t, scale = run(
        own_kernel, [shape(rows, width, BF16)] * 2 + [shape(rows, 128, F32)], student, teacher
    )
    block_s, block_t = run(
        functools.partial(early_kernel, starts(early[1:])),
        [block_shape] * 2,
        own_s,
        own_t,
        *raws(early[1:]),
    )
    once_s, product = run(
        functools.partial(lift_kernel, len(early) * rows),
        [shape(once_rows, width, BF16), shape(total, once_rows, F32)],
        block_s,
        *far_s[:n_once],
        flops=len(early) * once_rows * work,
    )
    mates = {k: across(once_s, k) for k in early[1:]}
    mates[0] = once_s
    for k in early:
        mates[k + 1] = across(mates[k], 1)

    for slots in (mid, last):
        block_s, block_t, product = run(
            functools.partial(more_kernel, starts(slots)),
            [block_shape, block_shape, shape(total, once_rows, F32)],
            block_s,
            block_t,
            product,
            once_s,
            *raws(slots),
            flops=len(slots) * once_rows * work,
            into=(0, 1, 2),
        )
    kept, sent, *back = run(
        functools.partial(once_kernel, n_once),
        [shape(half, once_rows, BF16)] * 2 + [shape(rows, width, BF16)] * n_once,
        block_s,
        block_t,
        product,
        *far_t[:n_once],
        flops=2 * n_gc * once_rows * work,
    )
    came = across(sent, 1)
    home = [along(b, n_gr - d) for b, d in zip(back, once)]
    n_pack = len(early)
    packed = run(
        functools.partial(pack_kernel, n_pack),
        [shape(rows, 2 * once_rows, BF16)] * n_pack + [shape(rows, width, BF16)] * len(late),
        kept,
        came,
        once_s,
        mates[1],
        flops=len(late) * 2 * once_rows * work,
    )
    weights = [packed[0]] + [across(p, k) for p, k in zip(packed[1:], early[1:])]
    home += [across(p, k) for p, k in zip(packed[n_pack:], late)]
    back = run(
        functools.partial(both_kernel, n_both),
        [shape(rows, width, BF16)] * n_both,
        block_s,
        block_t,
        *far_s[n_once:],
        *far_t[n_once:],
        flops=3 * n_both * n_gc * rows * work,
    )
    home += [along(b, n_gr - d) for b, d in zip(back, both)]
    (pull,) = run(
        near_kernel, [pull_shape], own_s, own_t, block_s, block_t, flops=3 * n_gc * rows * work
    )
    (pull,) = run(
        functools.partial(met_kernel, n_pack),
        [pull_shape],
        pull,
        *weights,
        *[mates[k + c] for k in early for c in (0, 1)],
        flops=n_gc * once_rows * work,
    )
    factor = 12.0 * (width / (rows * n_gr * n_gc)) ** 0.5
    return run(functools.partial(end_kernel, factor), [pull_shape], own_s, scale, pull, *home)[0]


def solution(mesh):
    n_gr, n_gc = mesh.shape["gr"], mesh.shape["gc"]
    spec = P(("gr", "gc"), None)

    def body(student, teacher):
        return local(n_gr, n_gc, student, teacher)

    return jax.shard_map(
        body, mesh=mesh, in_specs=(spec, spec), out_specs=spec, check_vma=False
    )
```

```python
import functools

import jax
import jax.numpy as jnp
from jax import lax
from jax.experimental import pallas as pl
from jax.experimental.pallas import tpu as pltpu
from jax.sharding import PartitionSpec as P


F32, BF16 = jnp.float32, jnp.bfloat16
VM = pl.BlockSpec(memory_space=pltpu.VMEM)


def inverse_rms(values):
    return lax.rsqrt(jnp.mean(values * values, axis=-1, keepdims=True) + 1e-06)


def unit_of(rows):
    values = rows.astype(F32)
    return (values * inverse_rms(values) * rows.shape[-1] ** (-0.5)).astype(BF16)


def nt(a, b):
    return lax.dot_general(a, b, (((1,), (1,)), ((), ())), preferred_element_type=F32)


def tn(a, b):
    return lax.dot_general(a, b, (((0,), (0,)), ((), ())), preferred_element_type=F32)


def nn(a, b):
    return lax.dot_general(a, b, (((1,), (0,)), ((), ())), preferred_element_type=F32)


def call(kernel, outs, *args, flops=0, into=()):
    size = sum(a.size * a.dtype.itemsize for a in args)
    size += sum(o.size * o.dtype.itemsize for o in outs)
    return pl.pallas_call(
        kernel,
        out_shape=outs,
        in_specs=[VM] * len(args),
        out_specs=[VM] * len(outs),
        input_output_aliases={i: i for i in into},
        cost_estimate=pl.CostEstimate(flops=flops, bytes_accessed=size, transcendentals=0),
        compiler_params=pltpu.CompilerParams(vmem_limit_bytes=24 << 20),
    )(*args)


def shape(rows, cols, dtype):
    return jax.ShapeDtypeStruct((rows, cols), dtype)


def store_units(out, starts, raws):
    for at, raw in zip(starts, raws):
        out[pl.ds(at, raw.shape[0]), :] = unit_of(raw[...])


def pull_of(rows_s, rows_t, block_s, block_t):
    stretch = 0.5 * rows_s.shape[1] ** 0.5
    sim = nt(block_s[...], rows_s) - nt(block_t[...], rows_t)
    return tn(jnp.tanh(stretch * sim).astype(BF16), block_s[...])


def own_kernel(student, teacher, unit_s, unit_t, scale):
    values = student[...].astype(F32)
    inverse = inverse_rms(values)
    unit_s[...] = (values * inverse * values.shape[-1] ** (-0.5)).astype(BF16)
    unit_t[...] = unit_of(teacher[...])
    scale[...] = jnp.broadcast_to(inverse, scale.shape)


def early_kernel(starts, own_s, own_t, *refs):
    *raws, block_s, block_t = refs
    n = len(starts)
    block_s[pl.ds(0, own_s.shape[0]), :] = own_s[...]
    block_t[pl.ds(0, own_s.shape[0]), :] = own_t[...]
    store_units(block_s, starts, raws[:n])
    store_units(block_t, starts, raws[n:])


def lift_kernel(size, block_s, *refs):
    *raws, once_s, product = refs
    rows = raws[0].shape[0]
    store_units(once_s, range(0, len(raws) * rows, rows), raws)
    at = pl.ds(0, size)
    product[at, :] = nt(block_s[at, :], once_s[...])


def more_kernel(starts, block_s, block_t, product, once_s, *refs):
    *raws, out_s, out_t, out = refs
    n = len(starts)
    rows = raws[0].shape[0]
    units = jnp.concatenate([unit_of(r[...]) for r in raws[:n]], axis=0)
    part = nt(units, once_s[...])
    for i, start in enumerate(starts):
        out_s[pl.ds(start, rows), :] = units[i * rows : (i + 1) * rows]
        out[pl.ds(start, rows), :] = part[i * rows : (i + 1) * rows]
    store_units(out_t, starts, raws[n:])


def once_kernel(n_once, block_s, block_t, product, *refs):
    raws, (kept, sent, *back) = refs[:n_once], refs[n_once:]
    stretch = 0.5 * block_t.shape[1] ** 0.5
    once_t = jnp.concatenate([unit_of(r[...]) for r in raws], axis=0)
    half = kept.shape[0]
    sums = None
    for start, out in ((half, sent), (0, kept)):
        at = pl.ds(start, half)
        sim = product[at, :] - nt(block_t[at, :], once_t)
        part = jnp.tanh(stretch * sim).astype(BF16)
        out[...] = part
        term = tn(part, block_s[at, :])
        sums = term if sums is None else sums + term
    rows = back[0].shape[0]
    for i, out in enumerate(back):
        out[...] = sums[i * rows : (i + 1) * rows].astype(BF16)


def both_kernel(n_both, block_s, block_t, *refs):
    raw_s, raw_t, back = refs[:n_both], refs[n_both : 2 * n_both], refs[2 * n_both :]
    for i in range(n_both):
        rows_s, rows_t = unit_of(raw_s[i][...]), unit_of(raw_t[i][...])
        back[i][...] = pull_of(rows_s, rows_t, block_s, block_t).astype(BF16)


def near_kernel(own_s, own_t, block_s, block_t, pull):
    pull[...] = pull_of(own_s[...], own_t[...], block_s, block_t)


def pack_kernel(n_pack, kept, came, once_s, mate_s, *outs):
    rows, half = outs[-1].shape[0], kept.shape[1]
    for k, out in enumerate(outs):
        at = pl.ds(k * rows, rows)
        if k < n_pack:
            out[:, pl.ds(0, half)] = kept[at, :]
            out[:, pl.ds(half, half)] = came[at, :]
        else:
            out[...] = (nn(kept[at, :], once_s[...]) + nn(came[at, :], mate_s[...])).astype(BF16)


def met_kernel(n, before, *refs):
    weights, units, pull = refs[:n], refs[n:-1], refs[-1]
    total = before[...]
    for k, weight in enumerate(weights):
        block = jnp.concatenate([units[2 * k][...], units[2 * k + 1][...]], axis=0)
        total += nn(weight[...], block)
    pull[...] = total


def end_kernel(factor, own_s, scale, *refs):
    *terms, out = refs
    unit = own_s[...].astype(F32)
    pull = terms[0][...]
    for term in terms[1:]:
        pull = pull + term[...].astype(F32)
    radial = jnp.sum(unit * pull, axis=-1, keepdims=True)
    out[...] = factor * scale[:, :1] * (pull - radial * unit)


def local(n_gr, n_gc, student, teacher):
    rows, width = student.shape
    axes = ("gr", "gc")

    def shift(x, pairs):
        return lax.ppermute(x, axes, pairs)

    def across(x, mask):
        pairs = [(g * n_gc + c, g * n_gc + (c ^ mask)) for g in range(n_gr) for c in range(n_gc)]
        return shift(x, pairs)

    order = []
    for i in range(n_gr):
        order.append(i // 2 if i % 2 == 0 else n_gr - 1 - i // 2)

    def along(x, step):
        pairs = []
        for i in range(n_gr):
            a, b = order[i], order[(i + step) % n_gr]
            pairs += [(a * n_gc + c, b * n_gc + c) for c in range(n_gc)]
        return shift(x, pairs)

    def run(kernel, outs, *args, flops=0, into=()):
        return call(kernel, outs, *args, flops=flops, into=into)

    once = list(range(1, (n_gr + 1) // 2))
    both = [n_gr // 2] if n_gr % 2 == 0 else []
    n_once, n_both = len(once), len(both)
    once_rows = n_once * rows
    far_s = [along(student, d) for d in once + both]
    far_t = [along(teacher, d) for d in once + both]

    even = list(range(0, n_gc, 2))
    early = [k for k in even if k & (k - 1) == 0]
    late = [k for k in even if k not in early]
    mid = [k + 1 for k in early]
    last = late + [k + 1 for k in late]
    half = rows * len(even)
    work = 2 * rows * width

    got_s, got_t = {0: student}, {0: teacher}
    for k in even[1:]:
        high = 1 << (k.bit_length() - 1)
        low = k & -k
        got_s[k] = across(got_s[k ^ high], high)
        got_t[k] = across(got_t[k ^ low], low)
    for k in even:
        got_s[k + 1] = across(got_s[k], 1)
        got_t[k + 1] = across(got_t[k], 1)

    def raws(slots):
        return [got_s[k] for k in slots] + [got_t[k] for k in slots]

    order_of = early + late
    place = {k: i * rows for i, k in enumerate(order_of + [k + 1 for k in order_of])}

    def starts(slots):
        return [place[k] for k in slots]

    total = n_gc * rows
    pull_shape = shape(rows, width, F32)
    block_shape = shape(total, width, BF16)
    own_s, own_t, scale = run(
        own_kernel, [shape(rows, width, BF16)] * 2 + [shape(rows, 128, F32)], student, teacher
    )
    block_s, block_t = run(
        functools.partial(early_kernel, starts(early[1:])),
        [block_shape] * 2,
        own_s,
        own_t,
        *raws(early[1:]),
    )
    once_s, product = run(
        functools.partial(lift_kernel, len(early) * rows),
        [shape(once_rows, width, BF16), shape(total, once_rows, F32)],
        block_s,
        *far_s[:n_once],
        flops=len(early) * once_rows * work,
    )
    mates = {k: across(once_s, k) for k in early[1:]}
    mates[0] = once_s
    for k in early:
        mates[k + 1] = across(mates[k], 1)

    for slots in (mid, last):
        block_s, block_t, product = run(
            functools.partial(more_kernel, starts(slots)),
            [block_shape, block_shape, shape(total, once_rows, F32)],
            block_s,
            block_t,
            product,
            once_s,
            *raws(slots),
            flops=len(slots) * once_rows * work,
            into=(0, 1, 2),
        )
    kept, sent, *back = run(
        functools.partial(once_kernel, n_once),
        [shape(half, once_rows, BF16)] * 2 + [shape(rows, width, BF16)] * n_once,
        block_s,
        block_t,
        product,
        *far_t[:n_once],
        flops=2 * n_gc * once_rows * work,
    )
    came = across(sent, 1)
    home = [along(b, n_gr - d) for b, d in zip(back, once)]
    n_pack = len(early)
    packed = run(
        functools.partial(pack_kernel, n_pack),
        [shape(rows, 2 * once_rows, BF16)] * n_pack + [shape(rows, width, BF16)] * len(late),
        kept,
        came,
        once_s,
        mates[1],
        flops=len(late) * 2 * once_rows * work,
    )
    weights = [packed[0]] + [across(p, k) for p, k in zip(packed[1:], early[1:])]
    home += [across(p, k) for p, k in zip(packed[n_pack:], late)]
    back = run(
        functools.partial(both_kernel, n_both),
        [shape(rows, width, BF16)] * n_both,
        block_s,
        block_t,
        *far_s[n_once:],
        *far_t[n_once:],
        flops=3 * n_both * n_gc * rows * work,
    )
    home += [along(b, n_gr - d) for b, d in zip(back, both)]
    (pull,) = run(
        near_kernel, [pull_shape], own_s, own_t, block_s, block_t, flops=3 * n_gc * rows * work
    )
    (pull,) = run(
        functools.partial(met_kernel, n_pack),
        [pull_shape],
        pull,
        *weights,
        *[mates[k + c] for k in early for c in (0, 1)],
        flops=n_gc * once_rows * work,
    )
    factor = 12.0 * (width / (rows * n_gr * n_gc)) ** 0.5
    return run(functools.partial(end_kernel, factor), [pull_shape], own_s, scale, pull, *home)[0]


def solution(mesh):
    n_gr, n_gc = mesh.shape["gr"], mesh.shape["gc"]
    spec = P(("gr", "gc"), None)

    def body(student, teacher):
        return local(n_gr, n_gc, student, teacher)

    return jax.shard_map(
        body, mesh=mesh, in_specs=(spec, spec), out_specs=spec, check_vma=False
    )
```
